32 devices in a mesh: fsdp: 4 (over y, x), ctx: 8 (over z, core).
Axes of the slice: x: 2, y: 2, z: 4, core: 2. Of those that a mesh axis runs over, the one named last changes fastest.
Arguments:
- inputs: bfloat16 [4, 2048, 768], P('fsdp', 'ctx'), may hold values from -6 to 6
- lengths: int32 [4], P('fsdp'), may hold values from 128 to 2048
- cotangent: bfloat16 [4, 2048, 768], P('fsdp', 'ctx'), may hold values from -6 to 6
- query_key_value: bfloat16 [768, 2304], P('fsdp'), may hold values from -0.21875 to 0.21875
- query_bias: bfloat16 [768], P('fsdp'), may hold values from -3 to 3
- value_bias: bfloat16 [768], P('fsdp'), may hold values from -0.125 to 0.125
- output_weight: bfloat16 [768, 768], P('fsdp'), may hold values from -3.5 to 3.5
- output_bias: bfloat16 [768], P('fsdp'), may hold values from -3 to 3
- first_gain: bfloat16 [768], P('fsdp'), may hold values from 0.5 to 1.5
- first_shift: bfloat16 [768], P('fsdp'), may hold values from -3 to 3
- hidden_weight: bfloat16 [768, 3072], P('fsdp'), may hold values from -0.21875 to 0.21875
- hidden_bias: bfloat16 [3072], P('fsdp'), may hold values from -3 to 3
- down_weight: bfloat16 [3072, 768], P('fsdp'), may hold values from -0.109375 to 0.109375
- down_bias: bfloat16 [768], P('fsdp'), may hold values from -3 to 3
- second_gain: bfloat16 [768], P('fsdp'), may hold values from 0.5 to 1.5
- second_shift: bfloat16 [768], P('fsdp'), may hold values from -3 to 3
Outputs:
- outputs: bfloat16 [4, 2048, 768], P('fsdp', 'ctx')
- input_grad: float32 [4, 2048, 768], P('fsdp', 'ctx')
- query_key_value_grad: float32 [768, 2304], P('fsdp')
- query_bias_grad: float32 [768], P('fsdp')
- value_bias_grad: float32 [768], P('fsdp')
- output_weight_grad: float32 [768, 768], P('fsdp')
- output_bias_grad: float32 [768], P('fsdp')
- first_gain_grad: float32 [768], P('fsdp')
- first_shift_grad: float32 [768], P('fsdp')
- hidden_weight_grad: float32 [768, 3072], P('fsdp')
- hidden_bias_grad: float32 [3072], P('fsdp')
- down_weight_grad: float32 [3072, 768], P('fsdp')
- down_bias_grad: float32 [768], P('fsdp')
- second_gain_grad: float32 [768], P('fsdp')
- second_shift_grad: float32 [768], P('fsdp')
The draws below stay inside these ranges and needn't reach their ends.
All inputs are finite; a program needn't handle non-finite values.
Results may differ from the reference program's by a relative error of at most 0.035.
Values may be sent and summed in bfloat16 or wider, within the bound.
No kernel may reach another device: no remote copies, remote signals or barrier semaphores. Data moves between devices by JAX's collectives and lax.ppermute only.
A program may use at most 128 MiB of HBM per device.

```python
import math
import jax
import jax.numpy as jnp
from jax import lax

D = 768
H = 12
HD = 64
FF = 3072
LENGTH = 2048
SEQS = 4


def place_ends(values, rng, least, largest):
    place = [jax.random.randint(jax.random.fold_in(rng, axis), (), 0, length) for axis, length in enumerate(values.shape)]
    main_axis = values.shape.index(max(values.shape))
    beside = place[:main_axis] + [(place[main_axis] + 1) % values.shape[main_axis]] + place[main_axis + 1:]
    return values.at[tuple(place)].set(least).at[tuple(beside)].set(largest)


def steps_of(own_key, extent, cuts, smallest, top_value):
    loudness, own = 1.0, jax.random.fold_in(own_key, 6)
    for axis_at, blocks in cuts:
        heights = jnp.exp(jax.random.uniform(jax.random.fold_in(own, axis_at), (blocks,), jnp.float32, smallest / len(cuts), top_value / len(cuts)))
        loudness = loudness * jnp.repeat(heights, extent[axis_at] // blocks).reshape([-1 if axis == axis_at else 1 for axis in range(len(extent))])
    return loudness


def noise(stream_key, shape, deviation, reach, pieces=(), held_as=jnp.bfloat16):
    array = jax.random.normal(stream_key, shape, jnp.float32) * deviation
    if len(pieces) > 0:
        array = steps_of(stream_key, shape, pieces, -0.22, 0.18) * array
    return jnp.clip(array, min=-reach, max=reach).astype(held_as)


def setup_inputs(seed: int = 0) -> dict:
    splits = jax.random.split(jax.random.key(seed), 17)
    inputs = noise(splits[0], (SEQS, LENGTH, D), 1.0, 6.0, ((0, 4), (1, 8)))
    lengths = place_ends(jax.random.randint(splits[1], (SEQS,), LENGTH // 16, LENGTH + 1), jax.random.fold_in(splits[1], 1), LENGTH // 16, LENGTH).astype(jnp.int32)
    cotangent = noise(splits[2], (SEQS, LENGTH, D), 1.0, 6.0, ((0, 4), (1, 8)))
    query_key_value = noise(splits[3], (D, 3 * D), D ** -0.5, 0.21875, ((0, 4),))
    query_bias = noise(splits[4], (D,), 0.5, 3.0, ((0, 4),))
    value_bias = noise(splits[5], (D,), 0.02, 0.125, ((0, 4),))
    output_weight = noise(splits[6], (D, D), (D * 6 // LENGTH + 1) ** -0.5, 3.5, ((0, 4),))
    output_bias = noise(splits[7], (D,), 0.5, 3.0, ((0, 4),))
    first_gain = jnp.clip(1.0 + 0.1 * jax.random.normal(splits[8], (D,), jnp.float32), 0.5, 1.5).astype(jnp.bfloat16)
    first_shift = noise(splits[9], (D,), 0.5, 3.0, ((0, 4),))
    hidden_weight = noise(splits[10], (D, FF), D ** -0.5, 0.21875, ((0, 4),))
    hidden_bias = noise(splits[11], (FF,), 0.5, 3.0, ((0, 4),))
    down_weight = noise(splits[12], (FF, D), FF ** -0.5, 0.109375, ((0, 4),))
    down_bias = noise(splits[13], (D,), 0.5, 3.0, ((0, 4),))
    second_gain = jnp.clip(1.0 + 0.1 * jax.random.normal(splits[14], (D,), jnp.float32), 0.5, 1.5).astype(jnp.bfloat16)
    second_shift = noise(splits[15], (D,), 0.5, 3.0, ((0, 4),))
    return dict(inputs=inputs, lengths=lengths, cotangent=cotangent, query_key_value=query_key_value, query_bias=query_bias, value_bias=value_bias, output_weight=output_weight, output_bias=output_bias, first_gain=first_gain, first_shift=first_shift, hidden_weight=hidden_weight, hidden_bias=hidden_bias, down_weight=down_weight, down_bias=down_bias, second_gain=second_gain, second_shift=second_shift)


PRECISE = lax.Precision.HIGHEST
EPSILON = 1e-12
MASKED = -1e+30

@jax.custom_vjp
def low(v):
    return lax.optimization_barrier(v.astype(jnp.bfloat16)).astype(jnp.float32)

@jax.custom_vjp
def low_back(v):
    return v

def low_keep(v):
    return (low(v), None)

def low_pass(kept, grad):
    return (grad,)

def back_keep(v):
    return (v, None)

def back_low(kept, grad):
    return (low(grad),)
low.defvjp(low_keep, low_pass)
low_back.defvjp(back_keep, back_low)

def matmul(left, right):
    return jnp.dot(left, right, precision=PRECISE)

def layer_norm(summed, norm_gain, norm_shift):
    row_mean = lax.optimization_barrier(jnp.mean(summed, axis=-1, keepdims=True))
    centred = summed - row_mean
    variance = lax.optimization_barrier(jnp.mean(centred * centred, axis=-1, keepdims=True))
    return centred * lax.rsqrt(variance + EPSILON) * norm_gain + norm_shift

def attend_block(query_block, keys, values, valid_keys):
    raw_scores = low_back(jnp.einsum('qhd,khd->hqk', query_block, keys, precision=PRECISE))
    scores = jnp.where(valid_keys[None, None, :], raw_scores * HD ** (-0.5), MASKED)
    row_max = lax.optimization_barrier(jnp.max(scores, axis=-1, keepdims=True))
    exponent = jnp.exp(scores - row_max)
    row_total = lax.optimization_barrier(jnp.sum(exponent, axis=-1))
    unnorm = low_back(jnp.einsum('hqk,khd->qhd', low(exponent), values, precision=PRECISE))
    return unnorm / jnp.transpose(row_total)[:, :, None]

def layer_apply(features, weights, length):
    joint_weight, query_bias, value_bias, output_weight, output_bias, first_gain, first_shift, hidden_weight, hidden_bias, down_weight, down_bias, second_gain, second_shift = weights
    joint_bias = jnp.concatenate([query_bias, jnp.zeros((D,), jnp.float32), value_bias])
    joint = low_back(low(matmul(features, joint_weight) + joint_bias))
    queries = joint[:, :D].reshape(LENGTH, H, HD)
    keys = joint[:, D:2 * D].reshape(LENGTH, H, HD)
    values = joint[:, 2 * D:].reshape(LENGTH, H, HD)
    valid_keys = jnp.arange(LENGTH, dtype=jnp.int32) < length
    block_size = math.gcd(LENGTH, 512)
    blocks = queries.reshape(LENGTH // block_size, block_size, H, HD)
    attended = lax.map(jax.checkpoint(lambda query_block: attend_block(query_block, keys, values, valid_keys)), blocks)
    attention = low(attended.reshape(LENGTH, D))
    branch = low_back(matmul(attention, output_weight) + output_bias)
    first = layer_norm(features + branch, first_gain, first_shift)
    pre_act = low_back(matmul(low(first), hidden_weight) + hidden_bias)
    activated = low(jax.nn.gelu(pre_act, approximate=False))
    down_out = low_back(matmul(activated, down_weight) + down_bias)
    return layer_norm(first + down_out, second_gain, second_shift)

def reference(inputs, lengths, cotangent, query_key_value, query_bias, value_bias, output_weight, output_bias, first_gain, first_shift, hidden_weight, hidden_bias, down_weight, down_bias, second_gain, second_shift):
    weights = tuple((entry.astype(jnp.float32) for entry in (query_key_value, query_bias, value_bias, output_weight, output_bias, first_gain, first_shift, hidden_weight, hidden_bias, down_weight, down_bias, second_gain, second_shift)))

    def one_sequence(carried, sliced):
        features, length, cotangent_seq = sliced
        layer_out, pullback = jax.vjp(lambda hidden_in, params: layer_apply(hidden_in, params, length), features, weights)
        feature_grad, weight_grads = pullback(cotangent_seq)
        return (jax.tree.map(jnp.add, carried, weight_grads), (layer_out.astype(jnp.bfloat16), feature_grad))
    initial = jax.tree.map(jnp.zeros_like, weights)
    totals, (outputs, input_grad) = lax.scan(one_sequence, initial, (inputs.astype(jnp.float32), lengths, cotangent.astype(jnp.float32)))
    return (outputs, input_grad, totals[0], totals[1], totals[2], totals[3], totals[4], totals[5], totals[6], totals[7], totals[8], totals[9], totals[10], totals[11], totals[12])
```

```python
import functools
import math

import jax
import jax.numpy as jnp
from jax import lax
from jax.experimental import pallas as pl
from jax.experimental.pallas import tpu as pltpu
from jax.sharding import PartitionSpec as P

H = 12
HD = 64
LANES = 128

EPSILON = 1e-12
MASKED = -1e30


def contract_rows(left, right):
    return lax.dot_general(
        left, right, (((0,), (0,)), ((), ())), preferred_element_type=jnp.float32
    )


def contract_cols(left, right):
    return lax.dot_general(
        left, right, (((1,), (1,)), ((), ())), preferred_element_type=jnp.float32
    )


def layer_norm(summed, norm_gain, norm_shift):
    row_mean = jnp.mean(summed, axis=-1, keepdims=True)
    centred = summed - row_mean
    variance = jnp.mean(centred * centred, axis=-1, keepdims=True)
    inv_std = lax.rsqrt(variance + EPSILON)
    scaled = centred * inv_std
    return (scaled * norm_gain + norm_shift, scaled, inv_std)


def norm_grad(out_grad, scaled, inv_std, norm_gain):
    gained = out_grad * norm_gain
    return inv_std * (
        gained
        - jnp.mean(gained, axis=-1, keepdims=True)
        - scaled * jnp.mean(gained * scaled, axis=-1, keepdims=True)
    )


def gelu_exact(values):
    return jax.nn.gelu(values, approximate=False)


def three_parts(column):
    high = column.astype(jnp.bfloat16).astype(jnp.float32)
    rest = column - high
    middle = rest.astype(jnp.bfloat16).astype(jnp.float32)
    return high, middle, rest - middle


def forward_kernel(q_ref, k_ref, v_ref, o_ref, q2_ref):
    q = q_ref[0]
    s = contract_cols(q, k_ref[0])
    row_max = jnp.max(s, axis=-1, keepdims=True)
    e = jnp.exp(s - row_max).astype(jnp.bfloat16)
    acc = jnp.dot(e, v_ref[0], preferred_element_type=jnp.float32)
    total = acc[:, HD : HD + 1]
    lane = lax.broadcasted_iota(jnp.int32, acc.shape, 1)
    o_ref[0] = jnp.where(lane < HD, acc / total, acc)
    high, middle, low = three_parts(-row_max)
    wide = jnp.where(
        lane == HD + 1,
        high,
        jnp.where(lane == HD + 2, middle, jnp.where(lane == HD + 3, low, q.astype(jnp.float32))),
    )
    q2_ref[0] = wide.astype(jnp.bfloat16)


def attend(q, k, v, block):
    heads, rows, _ = q.shape
    keys = k.shape[1]
    return pl.pallas_call(
        forward_kernel,
        grid=(heads, rows // block),
        in_specs=[
            pl.BlockSpec((1, block, LANES), lambda h, i: (h, i, 0)),
            pl.BlockSpec((1, keys, LANES), lambda h, i: (h, 0, 0)),
            pl.BlockSpec((1, keys, LANES), lambda h, i: (h, 0, 0)),
        ],
        out_specs=[
            pl.BlockSpec((1, block, LANES), lambda h, i: (h, i, 0)),
            pl.BlockSpec((1, block, LANES), lambda h, i: (h, i, 0)),
        ],
        out_shape=[
            jax.ShapeDtypeStruct((heads, rows, LANES), jnp.float32),
            jax.ShapeDtypeStruct((heads, rows, LANES), jnp.bfloat16),
        ],
        cost_estimate=pl.CostEstimate(
            flops=heads * rows * keys * 512,
            transcendentals=heads * rows * keys,
            bytes_accessed=heads * (rows + keys) * 1024,
        ),
    )(q, k, v)


def backward_kernel(
    q_ref, o_ref, g_ref, k_ref, kt_ref, v_ref, dq_ref, dk_ref, dv_ref, dk_acc, dv_acc, *, chunk
):
    step = pl.program_id(1)
    q = q_ref[0]
    o = o_ref[0]
    g = g_ref[0].astype(jnp.float32)
    total = o[:, HD : HD + 1]
    lane = lax.broadcasted_iota(jnp.int32, o.shape, 1)
    coef = jnp.sum(jnp.where(lane < HD, g * o, 0.0), axis=-1, keepdims=True) / total
    high, middle, low = three_parts(-coef)
    un = jnp.where(
        lane < HD,
        g / total,
        jnp.where(
            lane == HD,
            high,
            jnp.where(lane == HD + 1, middle, jnp.where(lane == HD + 2, low, 0.0)),
        ),
    ).astype(jnp.bfloat16)

    @pl.when(step == 0)
    def _():
        dk_acc[...] = jnp.zeros_like(dk_acc)
        dv_acc[...] = jnp.zeros_like(dv_acc)

    def keys_step(index, dq_sum):
        rows = pl.ds(pl.multiple_of(index * chunk, chunk), chunk)
        e = jnp.exp(contract_cols(k_ref[0, rows, :], q))
        gp = contract_cols(v_ref[0, rows, :], un)
        ds = (e * gp).astype(jnp.bfloat16)
        dv_acc[rows, :] += jnp.dot(
            e.astype(jnp.bfloat16), un, preferred_element_type=jnp.float32
        )
        dk_acc[rows, :] += jnp.dot(ds, q, preferred_element_type=jnp.float32)
        return dq_sum + jnp.dot(kt_ref[0, :, rows], ds, preferred_element_type=jnp.float32)

    steps = k_ref.shape[1] // chunk
    dq_t = lax.fori_loop(
        0, steps, keys_step, jnp.zeros((LANES, q.shape[0]), jnp.float32), unroll=steps <= 2
    )
    dq_ref[0] = (jnp.transpose(dq_t) * HD**-0.5).astype(jnp.bfloat16)

    @pl.when(step == pl.num_programs(1) - 1)
    def _():
        dk_ref[0] = dk_acc[...].astype(jnp.bfloat16)
        dv_ref[0] = dv_acc[...].astype(jnp.bfloat16)


def attend_back(q, o, g, k, v, block):
    heads, rows, _ = q.shape
    keys = k.shape[1]
    chunk = math.gcd(keys, 1024)
    rowwise = pl.BlockSpec((1, block, LANES), lambda h, i: (h, i, 0))
    keywise = pl.BlockSpec((1, keys, LANES), lambda h, i: (h, 0, 0))
    return pl.pallas_call(
        functools.partial(backward_kernel, chunk=chunk),
        grid=(heads, rows // block),
        in_specs=[
            rowwise,
            rowwise,
            rowwise,
            keywise,
            pl.BlockSpec((1, LANES, keys), lambda h, i: (h, 0, 0)),
            keywise,
        ],
        out_specs=[rowwise, keywise, keywise],
        out_shape=[
            jax.ShapeDtypeStruct((heads, rows, LANES), jnp.bfloat16),
            jax.ShapeDtypeStruct((heads, keys, LANES), jnp.bfloat16),
            jax.ShapeDtypeStruct((heads, keys, LANES), jnp.bfloat16),
        ],
        scratch_shapes=[
            pltpu.VMEM((keys, LANES), jnp.float32),
            pltpu.VMEM((keys, LANES), jnp.float32),
        ],
        cost_estimate=pl.CostEstimate(
            flops=heads * rows * keys * 1280,
            transcendentals=heads * rows * keys,
            bytes_accessed=heads * (rows + keys) * 1536,
        ),
    )(q, o, g, k, jnp.transpose(k, (0, 2, 1)), v)


def pick(stack, index):
    return lax.dynamic_index_in_dim(stack, index, 0, keepdims=False)


def body(
    inputs,
    lengths,
    cotangent,
    query_key_value,
    query_bias,
    value_bias,
    output_weight,
    output_bias,
    first_gain,
    first_shift,
    hidden_weight,
    hidden_bias,
    down_weight,
    down_bias,
    second_gain,
    second_shift,
):
    f32, bf16 = jnp.float32, jnp.bfloat16
    seqs, span, width = inputs.shape
    shards = lax.axis_size("fsdp")
    peers = lax.axis_size("ctx")
    groups = math.gcd(H, peers)
    copies = peers // groups
    planes = peers // 2
    heads = H // groups
    cols = heads * HD
    own_rows = query_key_value.shape[0]
    fsdp = lax.axis_index("fsdp")
    ctx = lax.axis_index("ctx")
    group, copy = ctx // copies, ctx % copies
    plane, core = ctx // 2, ctx % 2
    toks = seqs * span
    rows = groups * span
    keys = copies * rows
    ff = hidden_weight.shape[1]

    def move(value, axis, target):
        return lax.ppermute(
            value, axis, [(i, target(i)) for i in range(lax.axis_size(axis))]
        )

    def swap(value):
        return move(value, "ctx", lambda i: i ^ 1)

    def across(value, k):
        return move(value, "fsdp", lambda i: i ^ k)

    def to_group(value, d):
        return move(
            value, "ctx", lambda i: (i // copies + d) % groups * copies + i % copies
        )

    def to_copy(value, d):
        return move(
            value, "ctx", lambda i: i // copies * copies + (i % copies + d) % copies
        )

    def to_plane(value, d):
        return move(value, "ctx", lambda i: (i // 2 + d) % planes * 2 + i % 2)

    def gather_rows(shard):
        pieces = jnp.stack([shard] + [across(shard, k) for k in range(1, shards)])
        return jnp.concatenate([pick(pieces, fsdp ^ g) for g in range(shards)], axis=0)

    def gather_weight(shard):
        half = shard.shape[0] // 2
        mine = lax.dynamic_slice_in_dim(shard, core * half, half, 0)
        other = lax.dynamic_slice_in_dim(shard, (1 - core) * half, half, 0)
        near = [mine] + [across(mine, k) for k in range(1, shards)]
        far = [other] + [swap(piece) for piece in near[1:]]
        pieces = jnp.stack(near + far)
        ordered = []
        for g in range(shards):
            for side in range(2):
                ordered.append(pick(pieces, jnp.where(core == side, 0, shards) + (fsdp ^ g)))
        return jnp.concatenate(ordered, axis=0)

    own_cols = pick(
        query_key_value.reshape(own_rows, 3, groups, cols).transpose(2, 0, 1, 3), group
    ).reshape(own_rows, 3 * cols)
    w_joint = gather_rows(own_cols)
    vectors = jnp.stack(
        [
            query_bias,
            value_bias,
            output_bias,
            first_gain,
            first_shift,
            down_bias,
            second_gain,
            second_shift,
        ]
    )
    packed = jnp.concatenate([vectors, hidden_bias.reshape(-1, own_rows)], axis=0)
    packed = gather_rows(packed[None]).astype(f32)
    b_query, b_value, b_output, g_first, s_first, b_down, g_second, s_second = [
        packed[:, i].reshape(width) for i in range(8)
    ]
    b_hidden = packed[:, 8:].reshape(ff)

    x_all = jnp.concatenate(
        [inputs] + [to_group(inputs, d) for d in range(1, groups)], axis=1
    ).reshape(seqs * rows, width)

    w_output = gather_weight(output_weight)
    w_hidden = gather_weight(hidden_weight)
    w_down = gather_weight(down_weight)

    bias = jnp.concatenate(
        [
            lax.dynamic_slice_in_dim(b_query, group * cols, cols),
            jnp.zeros((cols,), f32),
            lax.dynamic_slice_in_dim(b_value, group * cols, cols),
        ]
    )
    joint = (jnp.dot(x_all, w_joint, preferred_element_type=f32) + bias).astype(bf16)
    joint = joint.reshape(seqs, rows, 3, heads, HD)
    kv_own = joint[:, :, 1:].reshape(seqs, rows, 2 * cols)
    kv = jnp.concatenate(
        [kv_own] + [to_copy(kv_own, d) for d in range(1, copies)], axis=1
    ).reshape(seqs, keys, 2, heads, HD)
    place = jnp.stack(
        [
            jnp.stack(
                [
                    (((group - d) % groups) * copies + (copy - e) % copies) * span
                    for d in range(groups)
                ]
            )
            for e in range(copies)
        ]
    )
    place = (place[:, :, None] + jnp.arange(span, dtype=jnp.int32)).reshape(keys)
    mask = jnp.where(place[None, :] < lengths[:, None], 0.0, MASKED).astype(bf16)

    def by_head(value):
        return value.transpose(0, 2, 1, 3).reshape(seqs * heads, value.shape[1], -1)

    def widen(value, *tail):
        head_rows = value.shape[:2]
        tail = [jnp.broadcast_to(t, head_rows + (t.shape[-1],)).astype(bf16) for t in tail]
        used = HD + sum(t.shape[-1] for t in tail)
        return jnp.concatenate(
            [value] + tail + [jnp.zeros(head_rows + (LANES - used,), bf16)], axis=-1
        )

    one = jnp.ones((1, 1, 1), bf16)
    three = jnp.ones((1, 1, 3), bf16)
    mask_heads = jnp.repeat(mask, heads, axis=0)[:, :, None]
    q_wide = widen(by_head(joint[:, :, 0]) * HD**-0.5, one)
    k_wide = widen(by_head(kv[:, :, 0]), mask_heads, three)
    v_wide = widen(by_head(kv[:, :, 1]), three)
    block = math.gcd(rows, 256)
    o_wide, q_wide = attend(q_wide, k_wide, v_wide, block)

    att_low = o_wide[:, :, :HD].astype(bf16).reshape(seqs, heads, groups, span, HD)
    att_low = att_low.transpose(2, 0, 3, 1, 4).reshape(groups, seqs, span, cols)
    got = jnp.stack(
        [att_low[0]] + [to_group(att_low[d], -d) for d in range(1, groups)]
    )
    attention_low = jnp.concatenate(
        [pick(got, (j - group) % groups) for j in range(groups)], axis=-1
    ).reshape(toks, width)

    tokens = inputs.reshape(toks, width).astype(f32)
    branch = jnp.dot(attention_low, w_output, preferred_element_type=f32) + b_output
    first_out, first_scaled, first_inv = layer_norm(tokens + branch, g_first, s_first)
    first_low = first_out.astype(bf16)
    pre_act = jnp.dot(first_low, w_hidden, preferred_element_type=f32) + b_hidden
    activated = gelu_exact(pre_act).astype(bf16)
    down_out = jnp.dot(activated, w_down, preferred_element_type=f32) + b_down
    second_out, second_scaled, second_inv = layer_norm(first_out + down_out, g_second, s_second)
    outputs = second_out.astype(bf16).reshape(seqs, span, width)
    out_grad = cotangent.reshape(toks, width).astype(f32)
    grad_second_gain = jnp.sum(out_grad * second_scaled, axis=0)
    grad_second_shift = jnp.sum(out_grad, axis=0)
    d_second = norm_grad(out_grad, second_scaled, second_inv, g_second)
    down_back = d_second.astype(bf16)
    grad_down_bias = jnp.sum(down_back.astype(f32), axis=0)
    act_grad = contract_cols(down_back, w_down)
    pre_back = jax.vjp(gelu_exact, pre_act)[1](act_grad)[0].astype(bf16)
    grad_hidden_bias = jnp.sum(pre_back.astype(f32), axis=0)
    d_first = contract_cols(pre_back, w_hidden) + d_second
    grad_first_gain = jnp.sum(d_first * first_scaled, axis=0)
    grad_first_shift = jnp.sum(d_first, axis=0)
    d_first_sum = norm_grad(d_first, first_scaled, first_inv, g_first)
    branch_back = d_first_sum.astype(bf16)
    grad_output_bias = jnp.sum(branch_back.astype(f32), axis=0)
    attention_back = contract_cols(branch_back, w_output).astype(bf16)

    parts = attention_back.reshape(seqs, span, groups, cols).transpose(2, 0, 1, 3)
    back = jnp.stack(
        [pick(parts, group)]
        + [to_group(pick(parts, (group + d) % groups), d) for d in range(1, groups)],
        axis=1,
    ).reshape(seqs, rows, heads, HD)
    g_wide = widen(by_head(back))

    grad_down = contract_rows(activated, down_back).astype(bf16)
    grad_hidden = contract_rows(first_low, pre_back).astype(bf16)
    grad_output = contract_rows(attention_low, branch_back).astype(bf16)

    def reduce_pair(grad):
        half = grad.shape[1] // 2
        grad = grad.reshape(shards, 2, half, -1).transpose(1, 0, 2, 3)
        return (pick(grad, core).astype(f32) + swap(pick(grad, 1 - core)).astype(f32)).astype(
            bf16
        )

    def reduce_shards(grad):
        total = pick(grad, fsdp).astype(f32)
        for k in range(1, shards):
            total = total + across(pick(grad, fsdp ^ k), k).astype(f32)
        return total.astype(bf16)

    def reduce_planes(grad):
        pieces = grad.reshape(planes, grad.shape[0] // planes, -1)
        total = pick(pieces, plane).astype(f32)
        for d in range(1, planes):
            total = total + to_plane(pick(pieces, (plane + d) % planes), d).astype(f32)
        total = total.astype(bf16)
        got = jnp.stack([total] + [to_plane(total, d) for d in range(1, planes)])
        return jnp.concatenate([pick(got, (plane - j) % planes) for j in range(planes)], axis=0)

    def join_pair(half):
        both = jnp.stack([half, swap(half)])
        return jnp.concatenate([pick(both, core), pick(both, 1 - core)], axis=0)

    def reduce_all(grad):
        return join_pair(reduce_planes(reduce_shards(reduce_pair(grad)))).astype(f32)

    small = jnp.stack(
        [
            grad_output_bias,
            grad_first_gain,
            grad_first_shift,
            grad_down_bias,
            grad_second_gain,
            grad_second_shift,
        ]
    ).reshape(6, shards, own_rows)
    small = jnp.concatenate(
        [small, grad_hidden_bias.reshape(shards, -1, own_rows).transpose(1, 0, 2)], axis=0
    )
    small_count = small.shape[0] * own_rows
    small = small.transpose(1, 0, 2).reshape(shards, small_count).astype(bf16)
    pad_rows = 64
    small = jnp.pad(small, ((0, 0), (0, pad_rows * width - small_count)))
    small = small.reshape(shards, pad_rows, width)
    total_down = reduce_all(grad_down.reshape(shards, ff // shards, width))
    total_hidden = reduce_all(grad_hidden.reshape(shards, own_rows, ff))
    total_rest = reduce_all(
        jnp.concatenate([grad_output.reshape(shards, own_rows, width), small], axis=1)
    )
    total_output = total_rest[:own_rows]
    flat = total_rest[own_rows:].reshape(-1)[:small_count].reshape(-1, own_rows)

    dq, dk, dv = attend_back(q_wide, o_wide, g_wide, k_wide, v_wide, block)
    dkv = jnp.stack([dk, dv])[..., :HD].reshape(2, seqs, heads, copies, rows, HD)
    dkv = dkv.transpose(3, 1, 4, 0, 2, 5).reshape(copies, seqs, rows, 2 * cols)
    kv_back = dkv[0].astype(f32)
    for d in range(1, copies):
        kv_back = kv_back + to_copy(dkv[d], -d).astype(f32)
    q_back = dq[..., :HD].reshape(seqs, heads, rows, HD).transpose(0, 2, 1, 3)
    joint_back = jnp.concatenate(
        [q_back.reshape(seqs, rows, cols), kv_back.astype(bf16)], axis=-1
    ).reshape(seqs * rows, 3 * cols)

    partial = contract_cols(joint_back, w_joint).astype(bf16).reshape(seqs, groups, span, width)
    input_grad = partial[:, 0].astype(f32) + d_first_sum.reshape(seqs, span, width)
    for d in range(1, groups):
        input_grad = input_grad + to_group(partial[:, d], -d).astype(f32)

    grad_joint = contract_rows(x_all, joint_back).astype(bf16).reshape(shards, own_rows, -1)
    sums = jnp.sum(joint_back.astype(f32), axis=0).reshape(3, cols)
    tail = jnp.zeros((2, width), f32)
    tail = lax.dynamic_update_slice(tail, sums[::2], (0, group * cols))
    tail = tail.reshape(2, shards, own_rows).transpose(1, 0, 2).reshape(shards, 1, -1)
    extra = 32
    tail = jnp.pad(
        tail.astype(bf16), ((0, 0), (0, extra - 1), (0, 3 * cols - tail.shape[-1]))
    )
    half = reduce_shards(reduce_pair(jnp.concatenate([grad_joint, tail], axis=1)))
    if copies > 2:
        total = half.astype(f32)
        for d in range(2, copies, 2):
            total = total + to_copy(half, d).astype(f32)
        half = total.astype(bf16)
    got = jnp.stack([half] + [to_group(half, d) for d in range(1, groups)])
    got = join_pair(got.transpose(1, 0, 2).reshape(half.shape[0], -1))
    got = got.reshape(own_rows + extra, groups, 3, cols).astype(f32)
    total_joint = jnp.stack(
        [
            lax.dynamic_index_in_dim(got, (group - j) % groups, 1, keepdims=False)
            for j in range(groups)
        ],
        axis=2,
    )[:own_rows].reshape(own_rows, 3 * width)
    biases = jnp.sum(got[own_rows].reshape(groups, -1), axis=0)

    return (
        outputs,
        input_grad,
        total_joint,
        biases[:own_rows],
        biases[own_rows : 2 * own_rows],
        total_output,
        flat[0],
        flat[1],
        flat[2],
        total_hidden,
        flat[6:].reshape(-1),
        total_down,
        flat[3],
        flat[4],
        flat[5],
    )


def solution(mesh):
    placed = (
        P("fsdp", "ctx", None),
        P("fsdp"),
        P("fsdp", "ctx", None),
        P("fsdp", None),
        P("fsdp"),
        P("fsdp"),
        P("fsdp", None),
        P("fsdp"),
        P("fsdp"),
        P("fsdp"),
        P("fsdp", None),
        P("fsdp"),
        P("fsdp", None),
        P("fsdp"),
        P("fsdp"),
        P("fsdp"),
    )
    return jax.shard_map(
        body,
        mesh=mesh,
        in_specs=placed,
        out_specs=(
            P("fsdp", "ctx", None),
            P("fsdp", "ctx", None),
            P("fsdp", None),
            P("fsdp"),
            P("fsdp"),
            P("fsdp", None),
            P("fsdp"),
            P("fsdp"),
            P("fsdp"),
            P("fsdp", None),
            P("fsdp"),
            P("fsdp", None),
            P("fsdp"),
            P("fsdp"),
            P("fsdp"),
        ),
        check_vma=False,
    )
```

```python
import functools
import math

import jax
import jax.numpy as jnp
from jax import lax
from jax.experimental import pallas as pl
from jax.experimental.pallas import tpu as pltpu
from jax.sharding import PartitionSpec as P


H = 12
HD = 64
LANES = 128

EPSILON = 1e-12
MASKED = -1e30


def contract_rows(left, right):
    return lax.dot_general(
        left, right, (((0,), (0,)), ((), ())), preferred_element_type=jnp.float32
    )


def contract_cols(left, right):
    return lax.dot_general(
        left, right, (((1,), (1,)), ((), ())), preferred_element_type=jnp.float32
    )


def layer_norm(summed, norm_gain, norm_shift):
    row_mean = jnp.mean(summed, axis=-1, keepdims=True)
    centred = summed - row_mean
    variance = jnp.mean(centred * centred, axis=-1, keepdims=True)
    inv_std = lax.rsqrt(variance + EPSILON)
    scaled = centred * inv_std
    return (scaled * norm_gain + norm_shift, scaled, inv_std)


def norm_grad(out_grad, scaled, inv_std, norm_gain):
    gained = out_grad * norm_gain
    return inv_std * (
        gained
        - jnp.mean(gained, axis=-1, keepdims=True)
        - scaled * jnp.mean(gained * scaled, axis=-1, keepdims=True)
    )


def gelu_exact(values):
    return jax.nn.gelu(values, approximate=False)


def three_parts(column):
    high = column.astype(jnp.bfloat16).astype(jnp.float32)
    rest = column - high
    middle = rest.astype(jnp.bfloat16).astype(jnp.float32)
    return high, middle, rest - middle


def forward_kernel(q_ref, own_ref, far_ref, low_ref, o_ref, q2_ref, *, heads):
    for h in range(heads):
        here = slice(h * LANES, (h + 1) * LANES)
        there = slice((heads + h) * LANES, (heads + h + 1) * LANES)
        q = q_ref[0, :, here]
        s_own = contract_cols(q, own_ref[0, :, here])
        s_far = contract_cols(q, far_ref[0, :, here])
        row_max = jnp.maximum(
            jnp.max(s_own, axis=-1, keepdims=True), jnp.max(s_far, axis=-1, keepdims=True)
        )
        e_own = jnp.exp(s_own - row_max).astype(jnp.bfloat16)
        e_far = jnp.exp(s_far - row_max).astype(jnp.bfloat16)
        acc = jnp.dot(e_own, own_ref[0, :, there], preferred_element_type=jnp.float32)
        acc += jnp.dot(e_far, far_ref[0, :, there], preferred_element_type=jnp.float32)
        total = acc[:, HD : HD + 1]
        lane = lax.broadcasted_iota(jnp.int32, acc.shape, 1)
        out = jnp.where(lane < HD, acc / total, acc)
        o_ref[0, :, here] = out
        low_ref[0, :, h * HD : (h + 1) * HD] = out[:, :HD].astype(jnp.bfloat16)
        high, middle, low = three_parts(-row_max)
        wide = jnp.where(
            lane == HD + 1,
            high,
            jnp.where(
                lane == HD + 2, middle, jnp.where(lane == HD + 3, low, q.astype(jnp.float32))
            ),
        )
        q2_ref[0, :, here] = wide.astype(jnp.bfloat16)


def attend(q, own, far, block):
    seqs, rows, wide = q.shape
    heads = wide // LANES
    keys = rows + far.shape[1]
    blockwise = pl.BlockSpec((1, block, wide), lambda s, i: (s, i, 0))
    return pl.pallas_call(
        functools.partial(forward_kernel, heads=heads),
        grid=(seqs, rows // block),
        in_specs=[
            blockwise,
            pl.BlockSpec((1, rows, 2 * wide), lambda s, i: (s, 0, 0)),
            pl.BlockSpec((1, far.shape[1], 2 * wide), lambda s, i: (s, 0, 0)),
        ],
        out_specs=[
            pl.BlockSpec((1, block, heads * HD), lambda s, i: (s, i, 0)),
            blockwise,
            blockwise,
        ],
        out_shape=[
            jax.ShapeDtypeStruct((seqs, rows, heads * HD), jnp.bfloat16),
            jax.ShapeDtypeStruct((seqs, rows, wide), jnp.float32),
            jax.ShapeDtypeStruct((seqs, rows, wide), jnp.bfloat16),
        ],
        cost_estimate=pl.CostEstimate(
            flops=seqs * heads * rows * keys * 512,
            transcendentals=seqs * heads * rows * keys,
            bytes_accessed=seqs * heads * (rows + keys) * 1024,
        ),
    )(q, own, far)


def backward_kernel(
    q_ref,
    o_ref,
    g_ref,
    k_own,
    v_own,
    k_far,
    v_far,
    dq_ref,
    dk_own,
    dv_own,
    dk_far,
    dv_far,
    dk_own_acc,
    dv_own_acc,
    dk_far_acc,
    dv_far_acc,
    *,
    head,
    chunk,
):
    step = pl.program_id(1)
    q = q_ref[0]
    o = o_ref[0]
    g = g_ref[0, :, head * HD : (head + 1) * HD].astype(jnp.float32)
    g = jnp.concatenate([g, jnp.zeros_like(g)], axis=-1)
    total = o[:, HD : HD + 1]
    lane = lax.broadcasted_iota(jnp.int32, o.shape, 1)
    coef = jnp.sum(g * o, axis=-1, keepdims=True) / total
    high, middle, low = three_parts(-coef)
    un = jnp.where(
        lane == HD,
        high,
        jnp.where(lane == HD + 1, middle, jnp.where(lane == HD + 2, low, g / total)),
    ).astype(jnp.bfloat16)
    dq_t = jnp.zeros((LANES, q.shape[0]), jnp.float32)
    last = step == pl.num_programs(1) - 1
    for k_ref, v_ref, dk_ref, dv_ref, dk_acc, dv_acc in (
        (k_own, v_own, dk_own, dv_own, dk_own_acc, dv_own_acc),
        (k_far, v_far, dk_far, dv_far, dk_far_acc, dv_far_acc),
    ):

        @pl.when(step == 0)
        def _():
            dk_acc[...] = jnp.zeros_like(dk_acc)
            dv_acc[...] = jnp.zeros_like(dv_acc)

        def keys_step(index, dq_sum):
            rows = pl.ds(pl.multiple_of(index * chunk, chunk), chunk)
            k = k_ref[0, rows, :]
            e = jnp.exp(contract_cols(k, q))
            gp = contract_cols(v_ref[0, rows, :], un)
            ds = (e * gp).astype(jnp.bfloat16)
            dv_acc[rows, :] += jnp.dot(
                e.astype(jnp.bfloat16), un, preferred_element_type=jnp.float32
            )
            dk_acc[rows, :] += jnp.dot(ds, q, preferred_element_type=jnp.float32)
            return dq_sum + contract_rows(k, ds)

        steps = k_ref.shape[1] // chunk
        dq_t = lax.fori_loop(0, steps, keys_step, dq_t, unroll=steps <= 2)

        @pl.when(last)
        def _():
            dk_ref[0] = dk_acc[...].astype(jnp.bfloat16)
            dv_ref[0] = dv_acc[...].astype(jnp.bfloat16)

    dq_ref[0] = jnp.transpose(dq_t).astype(jnp.bfloat16)


def attend_back(q, o, g, own, far, block, head):
    seqs, rows, wide = q.shape
    heads = wide // LANES
    distant = far.shape[1]
    chunk = math.gcd(rows, 1024)
    keys = rows + distant
    own_k = pl.BlockSpec((1, rows, LANES), lambda s, i: (s, 0, head))
    own_v = pl.BlockSpec((1, rows, LANES), lambda s, i: (s, 0, heads + head))
    far_k = pl.BlockSpec((1, distant, LANES), lambda s, i: (s, 0, head))
    far_v = pl.BlockSpec((1, distant, LANES), lambda s, i: (s, 0, heads + head))
    rowwise = pl.BlockSpec((1, block, LANES), lambda s, i: (s, i, head))
    near_out = pl.BlockSpec((1, rows, LANES), lambda s, i: (s, 0, 0))
    far_out = pl.BlockSpec((1, distant, LANES), lambda s, i: (s, 0, 0))
    near_shape = jax.ShapeDtypeStruct((seqs, rows, LANES), jnp.bfloat16)
    far_shape = jax.ShapeDtypeStruct((seqs, distant, LANES), jnp.bfloat16)
    return pl.pallas_call(
        functools.partial(backward_kernel, head=head, chunk=chunk),
        grid=(seqs, rows // block),
        in_specs=[
            rowwise,
            rowwise,
            pl.BlockSpec((1, block, heads * HD), lambda s, i: (s, i, 0)),
            own_k,
            own_v,
            far_k,
            far_v,
        ],
        out_specs=[
            pl.BlockSpec((1, block, LANES), lambda s, i: (s, i, 0)),
            near_out,
            near_out,
            far_out,
            far_out,
        ],
        out_shape=[near_shape, near_shape, near_shape, far_shape, far_shape],
        scratch_shapes=[
            pltpu.VMEM((rows, LANES), jnp.float32),
            pltpu.VMEM((rows, LANES), jnp.float32),
            pltpu.VMEM((distant, LANES), jnp.float32),
            pltpu.VMEM((distant, LANES), jnp.float32),
        ],
        cost_estimate=pl.CostEstimate(
            flops=seqs * rows * keys * 1280,
            transcendentals=seqs * rows * keys,
            bytes_accessed=seqs * (rows + keys) * 1536,
        ),
    )(q, o, g, own, own, far, far)


def pick(stack, index):
    return lax.dynamic_index_in_dim(stack, index, 0, keepdims=False)


def body(
    inputs,
    lengths,
    cotangent,
    query_key_value,
    query_bias,
    value_bias,
    output_weight,
    output_bias,
    first_gain,
    first_shift,
    hidden_weight,
    hidden_bias,
    down_weight,
    down_bias,
    second_gain,
    second_shift,
):
    f32, bf16 = jnp.float32, jnp.bfloat16
    seqs, span, width = inputs.shape
    shards = lax.axis_size("fsdp")
    peers = lax.axis_size("ctx")
    groups = math.gcd(H, peers)
    copies = peers // groups
    planes = peers // 2
    heads = H // groups
    cols = heads * HD
    own_rows = query_key_value.shape[0]
    fsdp = lax.axis_index("fsdp")
    ctx = lax.axis_index("ctx")
    group, copy = ctx // copies, ctx % copies
    plane, core = ctx // 2, ctx % 2
    toks = seqs * span
    rows = groups * span
    ff = hidden_weight.shape[1]

    def move(value, axis, target):
        return lax.ppermute(
            value, axis, [(i, target(i)) for i in range(lax.axis_size(axis))]
        )

    def swap(value):
        return move(value, "ctx", lambda i: i ^ 1)

    def across(value, k):
        return move(value, "fsdp", lambda i: i ^ k)

    def to_group(value, d):
        return move(
            value, "ctx", lambda i: (i // copies + d) % groups * copies + i % copies
        )

    def to_copy(value, d):
        return move(
            value, "ctx", lambda i: i // copies * copies + (i % copies + d) % copies
        )

    def to_plane(value, d):
        return move(value, "ctx", lambda i: (i // 2 + d) % planes * 2 + i % 2)

    def gather_rows(shard):
        pieces = jnp.stack([shard] + [across(shard, k) for k in range(1, shards)])
        return jnp.concatenate([pick(pieces, fsdp ^ g) for g in range(shards)], axis=0)

    def near_pieces(shard):
        half = shard.shape[0] // 2
        mine = lax.dynamic_slice_in_dim(shard, core * half, half, 0)
        return [mine] + [across(mine, k) for k in range(1, shards)]

    def finish_weight(shard, near):
        half = shard.shape[0] // 2
        other = lax.dynamic_slice_in_dim(shard, (1 - core) * half, half, 0)
        far = [other] + [swap(piece) for piece in near[1:]]
        pieces = jnp.stack(near + far)
        ordered = []
        for g in range(shards):
            for side in range(2):
                ordered.append(pick(pieces, jnp.where(core == side, 0, shards) + (fsdp ^ g)))
        return jnp.concatenate(ordered, axis=0)

    x_parts = [inputs] + [to_group(inputs, d) for d in range(1, groups)]

    own_cols = jnp.concatenate(
        [
            lax.dynamic_slice_in_dim(query_key_value, i * width + group * cols, cols, 1)
            for i in range(3)
        ],
        axis=1,
    )
    w_joint = gather_rows(own_cols).reshape(width, 3 * heads, HD)
    scale = jnp.where(jnp.arange(3 * heads) < heads, HD**-0.5, 1.0).astype(bf16)
    w_wide = jnp.pad(w_joint * scale[:, None], ((0, 0), (0, 0), (0, LANES - HD)))
    w_wide = w_wide.reshape(width, 3 * heads * LANES)

    w_output = gather_rows(output_weight)
    near_hidden = near_pieces(hidden_weight)
    near_down = near_pieces(down_weight)

    vectors = (
        query_bias,
        value_bias,
        output_bias,
        first_gain,
        first_shift,
        down_bias,
        second_gain,
        second_shift,
        hidden_bias,
    )
    vectors = lax.optimization_barrier(vectors + (x_parts[1],))
    x_parts[1] = vectors[9]
    packed = jnp.concatenate(
        [jnp.stack(vectors[:8]), vectors[8].reshape(-1, own_rows)], axis=0
    )
    packed = gather_rows(packed[None]).astype(f32)
    b_query, b_value, b_output, g_first, s_first, b_down, g_second, s_second = [
        packed[:, i].reshape(width) for i in range(8)
    ]
    b_hidden = packed[:, 8:].reshape(ff)

    x_all = jnp.concatenate(x_parts, axis=1).reshape(seqs * rows, width)

    place = jnp.stack(
        [(((group - d) % groups) * copies + copy) * span for d in range(groups)]
    )
    place = (place[:, None] + jnp.arange(span, dtype=jnp.int32)).reshape(rows)
    mask = jnp.where(place[None, :] < lengths[:, None], 0.0, MASKED).reshape(seqs * rows, 1)

    def wide_bias(value, ones):
        value = value.reshape(heads, HD)
        tail = jnp.zeros((LANES - HD,), f32).at[jnp.array(ones)].set(1.0)
        return jnp.concatenate(
            [value, jnp.broadcast_to(tail, (heads, LANES - HD))], axis=-1
        ).reshape(heads * LANES)

    wide = heads * LANES
    bias_q = wide_bias(
        lax.dynamic_slice_in_dim(b_query, group * cols, cols) * HD**-0.5, (0,)
    )
    bias_k = wide_bias(jnp.zeros((cols,), f32), (1, 2, 3))
    bias_v = wide_bias(lax.dynamic_slice_in_dim(b_value, group * cols, cols), (0, 1, 2))
    column = jnp.arange(2 * wide)
    masked = jnp.where((column < wide) & (column % LANES == HD), 1.0, 0.0)
    kv_own = (
        jnp.dot(x_all, w_wide[:, wide:], preferred_element_type=f32)
        + jnp.concatenate([bias_k, bias_v])
        + mask * masked
    ).astype(bf16)
    kv_own = kv_own.reshape(seqs, rows, 2 * wide)
    kv_far = [to_copy(kv_own, d) for d in range(1, copies)]
    kv_far = kv_far[0] if copies == 2 else jnp.concatenate(kv_far, axis=1)
    q_wide = (jnp.dot(x_all, w_wide[:, :wide], preferred_element_type=f32) + bias_q).astype(bf16)
    q_wide = q_wide.reshape(seqs, rows, wide)

    block = math.gcd(rows, 256)
    att_low, o_wide, q_wide = attend(q_wide, kv_own, kv_far, block)

    att_low, near_hidden, near_down = lax.optimization_barrier(
        (att_low, near_hidden, near_down)
    )
    att_low = att_low.reshape(seqs, groups, span, cols)
    got = jnp.stack(
        [att_low[:, 0]] + [to_group(att_low[:, d], -d) for d in range(1, groups)]
    )
    w_hidden = finish_weight(hidden_weight, near_hidden)
    w_down = finish_weight(down_weight, near_down)
    attention_low = jnp.concatenate(
        [pick(got, (j - group) % groups) for j in range(groups)], axis=-1
    ).reshape(toks, width)

    tokens = inputs.reshape(toks, width).astype(f32)
    branch = jnp.dot(attention_low, w_output, preferred_element_type=f32) + b_output
    first_out, first_scaled, first_inv = layer_norm(tokens + branch, g_first, s_first)
    first_low = first_out.astype(bf16)
    pre_act = jnp.dot(first_low, w_hidden, preferred_element_type=f32) + b_hidden
    activated = gelu_exact(pre_act).astype(bf16)
    down_out = jnp.dot(activated, w_down, preferred_element_type=f32) + b_down
    second_out, second_scaled, second_inv = layer_norm(first_out + down_out, g_second, s_second)
    outputs = second_out.astype(bf16).reshape(seqs, span, width)
    out_grad = cotangent.reshape(toks, width).astype(f32)
    grad_second_gain = jnp.sum(out_grad * second_scaled, axis=0)
    grad_second_shift = jnp.sum(out_grad, axis=0)
    d_second = norm_grad(out_grad, second_scaled, second_inv, g_second)
    down_back = d_second.astype(bf16)
    grad_down_bias = jnp.sum(down_back.astype(f32), axis=0)
    act_grad = contract_cols(down_back, w_down)
    pre_back = jax.vjp(gelu_exact, pre_act)[1](act_grad)[0].astype(bf16)
    grad_hidden_bias = jnp.sum(pre_back.astype(f32), axis=0)
    d_first = contract_cols(pre_back, w_hidden) + d_second
    grad_first_gain = jnp.sum(d_first * first_scaled, axis=0)
    grad_first_shift = jnp.sum(d_first, axis=0)
    d_first_sum = norm_grad(d_first, first_scaled, first_inv, g_first)
    branch_back = d_first_sum.astype(bf16)
    grad_output_bias = jnp.sum(branch_back.astype(f32), axis=0)
    attention_back = contract_cols(branch_back, w_output).astype(bf16)

    parts = attention_back.reshape(seqs, span, groups, cols).transpose(2, 0, 1, 3)
    g_all = jnp.concatenate(
        [pick(parts, group)]
        + [to_group(pick(parts, (group + d) % groups), d) for d in range(1, groups)],
        axis=1,
    )

    grad_down = contract_rows(activated, down_back).astype(bf16)
    grad_hidden = contract_rows(first_low, pre_back).astype(bf16)
    grad_output = contract_rows(attention_low, branch_back).astype(bf16)

    def reduce_pair(grad):
        half = grad.shape[1] // 2
        grad = grad.reshape(shards, 2, half, -1).transpose(1, 0, 2, 3)
        got = swap(pick(grad, 1 - core))
        return (pick(grad, core).astype(f32) + got.astype(f32)).astype(bf16)

    bits = shards.bit_length() - 1

    def reversed_bits(t):
        return sum(((t >> j) & 1) << (bits - 1 - j) for j in range(bits))

    def hyper(value, j):
        pairs = []
        for f in range(shards):
            for c in range(peers):
                bit = j if c % 2 == 0 else bits - 1 - j
                pairs.append((f * peers + c, (f ^ (1 << bit)) * peers + c))
        return lax.ppermute(value, ("fsdp", "ctx"), pairs)

    def reduce_shards(grad):
        held = {
            t: pick(grad, fsdp ^ jnp.where(core == 0, t, reversed_bits(t)))
            for t in range(shards)
        }
        for j in range(bits):
            sent = [t for t in held if (t >> j) & 1]
            got = hyper(jnp.stack([held.pop(t) for t in sent]), j)
            for i, t in enumerate(sent):
                kept = t ^ (1 << j)
                held[kept] = (held[kept].astype(f32) + got[i].astype(f32)).astype(bf16)
        return held[0]

    def reduce_planes(grad):
        pieces = grad.reshape(planes, grad.shape[0] // planes, -1)
        total = pick(pieces, plane).astype(f32)
        for d in range(1, planes):
            total = total + to_plane(pick(pieces, (plane + d) % planes), d).astype(f32)
        total = total.astype(bf16)
        got = jnp.stack([total] + [to_plane(total, d) for d in range(1, planes)])
        return jnp.concatenate([pick(got, (plane - j) % planes) for j in range(planes)], axis=0)

    def join_pair(half):
        both = jnp.stack([half, swap(half)])
        return jnp.concatenate([pick(both, core), pick(both, 1 - core)], axis=0)

    def reduce_all(grad):
        half = reduce_shards(reduce_pair(grad))
        return join_pair(reduce_planes(half)).astype(f32)

    small = jnp.stack(
        [
            grad_output_bias,
            grad_first_gain,
            grad_first_shift,
            grad_down_bias,
            grad_second_gain,
            grad_second_shift,
        ]
    ).reshape(6, shards, own_rows)
    small = jnp.concatenate(
        [small, grad_hidden_bias.reshape(shards, -1, own_rows).transpose(1, 0, 2)], axis=0
    )
    small_count = small.shape[0] * own_rows
    small = small.transpose(1, 0, 2).reshape(shards, small_count).astype(bf16)
    pad_rows = 64
    small = jnp.pad(small, ((0, 0), (0, pad_rows * width - small_count)))
    small = small.reshape(shards, pad_rows, width)
    total_down = reduce_all(grad_down.reshape(shards, ff // shards, width))
    total_hidden = reduce_all(grad_hidden.reshape(shards, own_rows, ff))
    total_rest = reduce_all(
        jnp.concatenate([grad_output.reshape(shards, own_rows, width), small], axis=1),
    )
    total_output = total_rest[:own_rows]
    flat = total_rest[own_rows:].reshape(-1)[:small_count].reshape(-1, own_rows)

    q_back, k_back, v_back = [], [], []
    for h in range(heads):
        dq, dk, dv, dk_far, dv_far = attend_back(q_wide, o_wide, g_all, kv_own, kv_far, block, h)
        q_back.append(dq)
        for parts, near, far in ((k_back, dk, dk_far), (v_back, dv, dv_far)):
            total = near.astype(f32)
            for d in range(1, copies):
                total = total + to_copy(far[:, (d - 1) * rows : d * rows], -d).astype(f32)
            parts.append(total.astype(bf16))
    joint_back = jnp.concatenate(q_back + k_back + v_back, axis=-1).reshape(seqs * rows, -1)

    partial = contract_cols(joint_back, w_wide).astype(bf16).reshape(seqs, groups, span, width)
    input_grad = partial[:, 0].astype(f32) + d_first_sum.reshape(seqs, span, width)
    for d in range(1, groups):
        input_grad = input_grad + to_group(partial[:, d], -d).astype(f32)

    unscale = jnp.where(jnp.arange(3 * heads) < heads, HD**-0.5, 1.0)[:, None]
    grad_joint = contract_rows(x_all, joint_back).reshape(width, 3 * heads, LANES)
    grad_joint = (grad_joint[..., :HD] * unscale).astype(bf16).reshape(shards, own_rows, -1)
    sums = jnp.sum(joint_back.astype(f32), axis=0).reshape(3 * heads, LANES)[:, :HD] * unscale
    sums = sums.reshape(3, cols)
    tail = jnp.zeros((2, width), f32)
    tail = lax.dynamic_update_slice(tail, sums[::2], (0, group * cols))
    tail = tail.reshape(2, shards, own_rows).transpose(1, 0, 2).reshape(shards, 1, -1)
    extra = 32
    tail = jnp.pad(
        tail.astype(bf16), ((0, 0), (0, extra - 1), (0, 3 * cols - tail.shape[-1]))
    )
    grad_joint = jnp.concatenate([grad_joint, tail], axis=1)
    half = reduce_shards(reduce_pair(grad_joint))
    if copies > 2:
        total = half.astype(f32)
        for d in range(2, copies, 2):
            total = total + to_copy(half, d).astype(f32)
        half = total.astype(bf16)
    got = jnp.stack([half] + [to_group(half, d) for d in range(1, groups)])
    got = join_pair(got.transpose(1, 0, 2).reshape(half.shape[0], -1))
    got = got.reshape(own_rows + extra, groups, 3, cols).astype(f32)
    total_joint = jnp.stack(
        [
            lax.dynamic_index_in_dim(got, (group - j) % groups, 1, keepdims=False)
            for j in range(groups)
        ],
        axis=2,
    )[:own_rows].reshape(own_rows, 3 * width)
    biases = jnp.sum(got[own_rows].reshape(groups, -1), axis=0)

    return (
        outputs,
        input_grad,
        total_joint,
        biases[:own_rows],
        biases[own_rows : 2 * own_rows],
        total_output,
        flat[0],
        flat[1],
        flat[2],
        total_hidden,
        flat[6:].reshape(-1),
        total_down,
        flat[3],
        flat[4],
        flat[5],
    )


def solution(mesh):
    placed = (
        P("fsdp", "ctx", None),
        P("fsdp"),
        P("fsdp", "ctx", None),
        P("fsdp", None),
        P("fsdp"),
        P("fsdp"),
        P("fsdp", None),
        P("fsdp"),
        P("fsdp"),
        P("fsdp"),
        P("fsdp", None),
        P("fsdp"),
        P("fsdp", None),
        P("fsdp"),
        P("fsdp"),
        P("fsdp"),
    )

    return jax.shard_map(
        body,
        mesh=mesh,
        in_specs=placed,
        out_specs=(
            P("fsdp", "ctx", None),
            P("fsdp", "ctx", None),
            P("fsdp", None),
            P("fsdp"),
            P("fsdp"),
            P("fsdp", None),
            P("fsdp"),
            P("fsdp"),
            P("fsdp"),
            P("fsdp", None),
            P("fsdp"),
            P("fsdp", None),
            P("fsdp"),
            P("fsdp"),
            P("fsdp"),
        ),
        check_vma=False,
    )
```

```python
import functools
import math

import jax
import jax.numpy as jnp
from jax import lax
from jax.experimental import pallas as pl
from jax.experimental.pallas import tpu as pltpu
from jax.sharding import PartitionSpec as P


H = 12
HD = 64
LANES = 128

EPSILON = 1e-12
MASKED = -1e30


def contract_rows(left, right):
    return lax.dot_general(
        left, right, (((0,), (0,)), ((), ())), preferred_element_type=jnp.float32
    )


def contract_cols(left, right):
    return lax.dot_general(
        left, right, (((1,), (1,)), ((), ())), preferred_element_type=jnp.float32
    )


def layer_norm(summed, norm_gain, norm_shift):
    row_mean = jnp.mean(summed, axis=-1, keepdims=True)
    centred = summed - row_mean
    variance = jnp.mean(centred * centred, axis=-1, keepdims=True)
    inv_std = lax.rsqrt(variance + EPSILON)
    scaled = centred * inv_std
    return (scaled * norm_gain + norm_shift, scaled, inv_std)


def norm_grad(out_grad, scaled, inv_std, norm_gain):
    gained = out_grad * norm_gain
    return inv_std * (
        gained
        - jnp.mean(gained, axis=-1, keepdims=True)
        - scaled * jnp.mean(gained * scaled, axis=-1, keepdims=True)
    )


def gelu_exact(values):
    return jax.nn.gelu(values, approximate=False)


def three_parts(column):
    high = column.astype(jnp.bfloat16).astype(jnp.float32)
    rest = column - high
    middle = rest.astype(jnp.bfloat16).astype(jnp.float32)
    return high, middle, rest - middle


def forward_kernel(q_ref, own_ref, far_ref, low_ref, o_ref, q2_ref, *, heads):
    for h in range(heads):
        here = slice(h * LANES, (h + 1) * LANES)
        there = slice((heads + h) * LANES, (heads + h + 1) * LANES)
        q = q_ref[0, :, here]
        s_own = contract_cols(q, own_ref[0, :, here])
        s_far = contract_cols(q, far_ref[0, :, here])
        row_max = jnp.maximum(
            jnp.max(s_own, axis=-1, keepdims=True), jnp.max(s_far, axis=-1, keepdims=True)
        )
        e_own = jnp.exp(s_own - row_max).astype(jnp.bfloat16)
        e_far = jnp.exp(s_far - row_max).astype(jnp.bfloat16)
        acc = jnp.dot(e_own, own_ref[0, :, there], preferred_element_type=jnp.float32)
        acc += jnp.dot(e_far, far_ref[0, :, there], preferred_element_type=jnp.float32)
        total = acc[:, HD : HD + 1]
        lane = lax.broadcasted_iota(jnp.int32, acc.shape, 1)
        out = jnp.where(lane < HD, acc / total, acc)
        o_ref[0, :, here] = out
        low_ref[0, :, h * HD : (h + 1) * HD] = out[:, :HD].astype(jnp.bfloat16)
        high, middle, low = three_parts(-row_max)
        wide = jnp.where(
            lane == HD + 1,
            high,
            jnp.where(
                lane == HD + 2, middle, jnp.where(lane == HD + 3, low, q.astype(jnp.float32))
            ),
        )
        q2_ref[0, :, here] = wide.astype(jnp.bfloat16)


def attend(q, own, far, block):
    seqs, rows, wide = q.shape
    heads = wide // LANES
    keys = rows + far.shape[1]
    blockwise = pl.BlockSpec((1, block, wide), lambda s, i: (s, i, 0))
    return pl.pallas_call(
        functools.partial(forward_kernel, heads=heads),
        grid=(seqs, rows // block),
        in_specs=[
            blockwise,
            pl.BlockSpec((1, rows, 2 * wide), lambda s, i: (s, 0, 0)),
            pl.BlockSpec((1, far.shape[1], 2 * wide), lambda s, i: (s, 0, 0)),
        ],
        out_specs=[
            pl.BlockSpec((1, block, heads * HD), lambda s, i: (s, i, 0)),
            blockwise,
            blockwise,
        ],
        out_shape=[
            jax.ShapeDtypeStruct((seqs, rows, heads * HD), jnp.bfloat16),
            jax.ShapeDtypeStruct((seqs, rows, wide), jnp.float32),
            jax.ShapeDtypeStruct((seqs, rows, wide), jnp.bfloat16),
        ],
        cost_estimate=pl.CostEstimate(
            flops=seqs * heads * rows * keys * 512,
            transcendentals=seqs * heads * rows * keys,
            bytes_accessed=seqs * heads * (rows + keys) * 1024,
        ),
    )(q, own, far)


def backward_kernel(
    q_ref,
    o_ref,
    g_ref,
    k_own,
    v_own,
    k_far,
    v_far,
    dq_ref,
    dk_own,
    dv_own,
    dk_far,
    dv_far,
    dk_own_acc,
    dv_own_acc,
    dk_far_acc,
    dv_far_acc,
    *,
    head,
    chunk,
):
    step = pl.program_id(1)
    q = q_ref[0]
    o = o_ref[0]
    g = g_ref[0, :, head * HD : (head + 1) * HD].astype(jnp.float32)
    g = jnp.concatenate([g, jnp.zeros_like(g)], axis=-1)
    total = o[:, HD : HD + 1]
    lane = lax.broadcasted_iota(jnp.int32, o.shape, 1)
    coef = jnp.sum(g * o, axis=-1, keepdims=True) / total
    high, middle, low = three_parts(-coef)
    un = jnp.where(
        lane == HD,
        high,
        jnp.where(lane == HD + 1, middle, jnp.where(lane == HD + 2, low, g / total)),
    ).astype(jnp.bfloat16)
    dq_t = jnp.zeros((LANES, q.shape[0]), jnp.float32)
    last = step == pl.num_programs(1) - 1
    for k_ref, v_ref, dk_ref, dv_ref, dk_acc, dv_acc in (
        (k_own, v_own, dk_own, dv_own, dk_own_acc, dv_own_acc),
        (k_far, v_far, dk_far, dv_far, dk_far_acc, dv_far_acc),
    ):

        @pl.when(step == 0)
        def _():
            dk_acc[...] = jnp.zeros_like(dk_acc)
            dv_acc[...] = jnp.zeros_like(dv_acc)

        def keys_step(index, dq_sum):
            rows = pl.ds(pl.multiple_of(index * chunk, chunk), chunk)
            k = k_ref[0, rows, :]
            e = jnp.exp(contract_cols(k, q))
            gp = contract_cols(v_ref[0, rows, :], un)
            ds = (e * gp).astype(jnp.bfloat16)
            dv_acc[rows, :] += jnp.dot(
                e.astype(jnp.bfloat16), un, preferred_element_type=jnp.float32
            )
            dk_acc[rows, :] += jnp.dot(ds, q, preferred_element_type=jnp.float32)
            return dq_sum + contract_rows(k, ds)

        steps = k_ref.shape[1] // chunk
        dq_t = lax.fori_loop(0, steps, keys_step, dq_t, unroll=steps <= 2)

        @pl.when(last)
        def _():
            dk_ref[0] = dk_acc[...].astype(jnp.bfloat16)
            dv_ref[0] = dv_acc[...].astype(jnp.bfloat16)

    dq_ref[0] = jnp.transpose(dq_t).astype(jnp.bfloat16)


def attend_back(q, o, g, own, far, block, head):
    seqs, rows, wide = q.shape
    heads = wide // LANES
    distant = far.shape[1]
    chunk = math.gcd(rows, 1024)
    keys = rows + distant
    own_k = pl.BlockSpec((1, rows, LANES), lambda s, i: (s, 0, head))
    own_v = pl.BlockSpec((1, rows, LANES), lambda s, i: (s, 0, heads + head))
    far_k = pl.BlockSpec((1, distant, LANES), lambda s, i: (s, 0, head))
    far_v = pl.BlockSpec((1, distant, LANES), lambda s, i: (s, 0, heads + head))
    rowwise = pl.BlockSpec((1, block, LANES), lambda s, i: (s, i, head))
    near_out = pl.BlockSpec((1, rows, LANES), lambda s, i: (s, 0, 0))
    far_out = pl.BlockSpec((1, distant, LANES), lambda s, i: (s, 0, 0))
    near_shape = jax.ShapeDtypeStruct((seqs, rows, LANES), jnp.bfloat16)
    far_shape = jax.ShapeDtypeStruct((seqs, distant, LANES), jnp.bfloat16)
    return pl.pallas_call(
        functools.partial(backward_kernel, head=head, chunk=chunk),
        grid=(seqs, rows // block),
        in_specs=[
            rowwise,
            rowwise,
            pl.BlockSpec((1, block, heads * HD), lambda s, i: (s, i, 0)),
            own_k,
            own_v,
            far_k,
            far_v,
        ],
        out_specs=[
            pl.BlockSpec((1, block, LANES), lambda s, i: (s, i, 0)),
            near_out,
            near_out,
            far_out,
            far_out,
        ],
        out_shape=[near_shape, near_shape, near_shape, far_shape, far_shape],
        scratch_shapes=[
            pltpu.VMEM((rows, LANES), jnp.float32),
            pltpu.VMEM((rows, LANES), jnp.float32),
            pltpu.VMEM((distant, LANES), jnp.float32),
            pltpu.VMEM((distant, LANES), jnp.float32),
        ],
        cost_estimate=pl.CostEstimate(
            flops=seqs * rows * keys * 1280,
            transcendentals=seqs * rows * keys,
            bytes_accessed=seqs * (rows + keys) * 1536,
        ),
    )(q, o, g, own, own, far, far)


def pick(stack, index):
    return lax.dynamic_index_in_dim(stack, index, 0, keepdims=False)


def body(
    inputs,
    lengths,
    cotangent,
    query_key_value,
    query_bias,
    value_bias,
    output_weight,
    output_bias,
    first_gain,
    first_shift,
    hidden_weight,
    hidden_bias,
    down_weight,
    down_bias,
    second_gain,
    second_shift,
):
    f32, bf16 = jnp.float32, jnp.bfloat16
    seqs, span, width = inputs.shape
    shards = lax.axis_size("fsdp")
    peers = lax.axis_size("ctx")
    groups = math.gcd(H, peers)
    copies = peers // groups
    planes = peers // 2
    heads = H // groups
    cols = heads * HD
    own_rows = query_key_value.shape[0]
    fsdp = lax.axis_index("fsdp")
    ctx = lax.axis_index("ctx")
    group, copy = ctx // copies, ctx % copies
    plane, core = ctx // 2, ctx % 2
    toks = seqs * span
    rows = groups * span
    ff = hidden_weight.shape[1]

    def move(value, axis, target):
        return lax.ppermute(
            value, axis, [(i, target(i)) for i in range(lax.axis_size(axis))]
        )

    def swap(value):
        return move(value, "ctx", lambda i: i ^ 1)

    def across(value, k):
        return move(value, "fsdp", lambda i: i ^ k)

    def to_group(value, d):
        return move(
            value, "ctx", lambda i: (i // copies + d) % groups * copies + i % copies
        )

    def to_copy(value, d):
        return move(
            value, "ctx", lambda i: i // copies * copies + (i % copies + d) % copies
        )

    def to_plane(value, d):
        return move(value, "ctx", lambda i: (i // 2 + d) % planes * 2 + i % 2)

    def gather_rows(shard):
        pieces = jnp.stack([shard] + [across(shard, k) for k in range(1, shards)])
        return jnp.concatenate([pick(pieces, fsdp ^ g) for g in range(shards)], axis=0)

    def near_pieces(mine):
        pieces = [mine]
        for k in range(1, shards):
            pieces.append(across(mine, k))
        return pieces

    def own_half(shard):
        half = shard.shape[0] // 2
        return lax.dynamic_slice_in_dim(shard, core * half, half, 0)

    def finish_weight(shard, near):
        half = shard.shape[0] // 2
        other = lax.dynamic_slice_in_dim(shard, (1 - core) * half, half, 0)
        far = [other]
        for piece in near[1:]:
            far.append(swap(piece))
        pieces = jnp.stack(near + far)
        ordered = []
        for g in range(shards):
            for side in range(2):
                ordered.append(pick(pieces, jnp.where(core == side, 0, shards) + (fsdp ^ g)))
        return jnp.concatenate(ordered, axis=0)

    x_parts = [inputs] + [to_group(inputs, d) for d in range(1, groups)]

    own_cols = jnp.concatenate(
        [
            lax.dynamic_slice_in_dim(query_key_value, i * width + group * cols, cols, 1)
            for i in range(3)
        ],
        axis=1,
    )
    w_joint = gather_rows(own_cols).reshape(width, 3 * heads, HD)
    scale = jnp.where(jnp.arange(3 * heads) < heads, HD**-0.5, 1.0).astype(bf16)
    w_joint = w_joint * scale[:, None]
    w_wide = jnp.pad(w_joint, ((0, 0), (0, 0), (0, LANES - HD)))
    w_wide = w_wide.reshape(width, 3 * heads * LANES)

    near_output = near_pieces(output_weight)
    near_hidden = near_pieces(own_half(hidden_weight))
    near_down = near_pieces(own_half(down_weight))

    vectors = (
        query_bias,
        value_bias,
        output_bias,
        first_gain,
        first_shift,
        down_bias,
        second_gain,
        second_shift,
        hidden_bias,
    )
    vectors = lax.optimization_barrier(vectors + (x_parts[1],))
    x_parts[1] = vectors[9]
    packed = jnp.concatenate(
        [jnp.stack(vectors[:8]), vectors[8].reshape(-1, own_rows)], axis=0
    )
    packed = gather_rows(packed[None]).astype(f32)
    b_query, b_value, b_output, g_first, s_first, b_down, g_second, s_second = [
        packed[:, i].reshape(width) for i in range(8)
    ]
    b_hidden = packed[:, 8:].reshape(ff)

    x_all = jnp.concatenate(x_parts, axis=1).reshape(seqs * rows, width)

    place = jnp.stack(
        [(((group - d) % groups) * copies + copy) * span for d in range(groups)]
    )
    place = (place[:, None] + jnp.arange(span, dtype=jnp.int32)).reshape(rows)
    mask = jnp.where(place[None, :] < lengths[:, None], 0.0, MASKED).reshape(seqs * rows, 1)

    def wide_bias(value, ones):
        value = value.reshape(heads, HD)
        tail = jnp.zeros((LANES - HD,), f32).at[jnp.array(ones)].set(1.0)
        return jnp.concatenate(
            [value, jnp.broadcast_to(tail, (heads, LANES - HD))], axis=-1
        ).reshape(heads * LANES)

    wide = heads * LANES
    bias_q = wide_bias(
        lax.dynamic_slice_in_dim(b_query, group * cols, cols) * HD**-0.5, (0,)
    )
    bias_k = wide_bias(jnp.zeros((cols,), f32), (1, 2, 3))
    bias_v = wide_bias(lax.dynamic_slice_in_dim(b_value, group * cols, cols), (0, 1, 2))
    column = jnp.arange(2 * wide)
    masked = jnp.where((column < wide) & (column % LANES == HD), 1.0, 0.0)
    kv_own = (
        jnp.dot(x_all, w_wide[:, wide:], preferred_element_type=f32)
        + jnp.concatenate([bias_k, bias_v])
        + mask * masked
    ).astype(bf16)
    kv_own = kv_own.reshape(seqs, rows, 2 * wide)
    kv_far = [to_copy(kv_own, d) for d in range(1, copies)]
    kv_far = kv_far[0] if copies == 2 else jnp.concatenate(kv_far, axis=1)
    q_wide = (jnp.dot(x_all, w_wide[:, :wide], preferred_element_type=f32) + bias_q).astype(bf16)
    q_wide = q_wide.reshape(seqs, rows, wide)

    block = math.gcd(rows, 256)
    att_low, o_wide, q_wide = attend(q_wide, kv_own, kv_far, block)

    att_low, near_hidden, near_down, near_output = lax.optimization_barrier(
        (att_low, near_hidden, near_down, near_output)
    )
    att_low = att_low.reshape(seqs, groups, span, cols)
    got = [att_low[:, 0]]
    for d in range(1, groups):
        got.append(to_group(att_low[:, d], -d))
    got = jnp.stack(got)
    pieces = jnp.stack(near_output)
    w_output = jnp.concatenate([pick(pieces, fsdp ^ g) for g in range(shards)], axis=0)
    w_hidden = finish_weight(hidden_weight, near_hidden)
    w_down = finish_weight(down_weight, near_down)
    attention_low = jnp.concatenate(
        [pick(got, (j - group) % groups) for j in range(groups)], axis=-1
    ).reshape(toks, width)

    tokens = inputs.reshape(toks, width).astype(f32)
    branch = jnp.dot(attention_low, w_output, preferred_element_type=f32) + b_output
    first_out, first_scaled, first_inv = layer_norm(tokens + branch, g_first, s_first)
    first_low = first_out.astype(bf16)
    pre_act = jnp.dot(first_low, w_hidden, preferred_element_type=f32) + b_hidden
    activated = gelu_exact(pre_act).astype(bf16)
    down_out = jnp.dot(activated, w_down, preferred_element_type=f32) + b_down
    second_out, second_scaled, second_inv = layer_norm(first_out + down_out, g_second, s_second)
    outputs = second_out.astype(bf16).reshape(seqs, span, width)
    out_grad = cotangent.reshape(toks, width).astype(f32)
    grad_second_gain = jnp.sum(out_grad * second_scaled, axis=0)
    grad_second_shift = jnp.sum(out_grad, axis=0)
    d_second = norm_grad(out_grad, second_scaled, second_inv, g_second)
    down_back = d_second.astype(bf16)
    grad_down_bias = jnp.sum(down_back.astype(f32), axis=0)
    act_grad = contract_cols(down_back, w_down)
    pre_back = jax.vjp(gelu_exact, pre_act)[1](act_grad)[0].astype(bf16)
    grad_hidden_bias = jnp.sum(pre_back.astype(f32), axis=0)
    d_first = contract_cols(pre_back, w_hidden) + d_second
    grad_first_gain = jnp.sum(d_first * first_scaled, axis=0)
    grad_first_shift = jnp.sum(d_first, axis=0)
    d_first_sum = norm_grad(d_first, first_scaled, first_inv, g_first)
    branch_back = d_first_sum.astype(bf16)
    grad_output_bias = jnp.sum(branch_back.astype(f32), axis=0)
    attention_back = contract_cols(branch_back, w_output).astype(bf16)

    parts = attention_back.reshape(seqs, span, groups, cols).transpose(2, 0, 1, 3)
    g_all = [pick(parts, group)]
    for d in range(1, groups):
        sent = pick(parts, (group + d) % groups)
        g_all.append(to_group(sent, d))
    g_all = jnp.concatenate(g_all, axis=1)

    grad_down = contract_rows(activated, down_back).astype(bf16)
    grad_hidden = contract_rows(first_low, pre_back).astype(bf16)
    grad_output = contract_rows(attention_low, branch_back).astype(bf16)

    def reduce_pair(grad):
        half = grad.shape[1] // 2
        grad = grad.reshape(shards, 2, half, -1).transpose(1, 0, 2, 3)
        got = swap(pick(grad, 1 - core))
        return (pick(grad, core).astype(f32) + got.astype(f32)).astype(bf16)

    bits = shards.bit_length() - 1

    def reversed_bits(t):
        return sum(((t >> j) & 1) << (bits - 1 - j) for j in range(bits))

    def hyper(value, j):
        pairs = []
        for f in range(shards):
            for c in range(peers):
                bit = j if c % 2 == 0 else bits - 1 - j
                pairs.append((f * peers + c, (f ^ (1 << bit)) * peers + c))
        return lax.ppermute(value, ("fsdp", "ctx"), pairs)

    def reduce_shards(grad):
        held = {
            t: pick(grad, fsdp ^ jnp.where(core == 0, t, reversed_bits(t)))
            for t in range(shards)
        }
        for j in range(bits):
            sent = [t for t in held if (t >> j) & 1]
            got = hyper(jnp.stack([held.pop(t) for t in sent]), j)
            for i, t in enumerate(sent):
                kept = t ^ (1 << j)
                held[kept] = (held[kept].astype(f32) + got[i].astype(f32)).astype(bf16)
        return held[0]

    def reduce_planes(grad):
        pieces = grad.reshape(planes, grad.shape[0] // planes, -1)
        total = pick(pieces, plane).astype(f32)
        for d in range(1, planes):
            sent = pick(pieces, (plane + d) % planes)
            got = to_plane(sent, d)
            total = total + got.astype(f32)
        total = total.astype(bf16)
        got = [total]
        for d in range(1, planes):
            got.append(to_plane(total, d))
        got = jnp.stack(got)
        return jnp.concatenate([pick(got, (plane - j) % planes) for j in range(planes)], axis=0)

    def join_pair(half):
        both = jnp.stack([half, swap(half)])
        return jnp.concatenate([pick(both, core), pick(both, 1 - core)], axis=0)

    def reduce_all(grad):
        half = reduce_shards(reduce_pair(grad))
        return join_pair(reduce_planes(half)).astype(f32)

    small = jnp.stack(
        [
            grad_output_bias,
            grad_first_gain,
            grad_first_shift,
            grad_down_bias,
            grad_second_gain,
            grad_second_shift,
        ]
    ).reshape(6, shards, own_rows)
    small = jnp.concatenate(
        [small, grad_hidden_bias.reshape(shards, -1, own_rows).transpose(1, 0, 2)], axis=0
    )
    small_count = small.shape[0] * own_rows
    small = small.transpose(1, 0, 2).reshape(shards, small_count).astype(bf16)
    pad_rows = 64
    small = jnp.pad(small, ((0, 0), (0, pad_rows * width - small_count)))
    small = small.reshape(shards, pad_rows, width)
    total_down = reduce_all(grad_down.reshape(shards, ff // shards, width))
    total_hidden = reduce_all(grad_hidden.reshape(shards, own_rows, ff))
    total_rest = reduce_all(
        jnp.concatenate([grad_output.reshape(shards, own_rows, width), small], axis=1),
    )
    total_output = total_rest[:own_rows]
    flat = total_rest[own_rows:].reshape(-1)[:small_count].reshape(-1, own_rows)

    q_back, k_back, v_back = [], [], []
    for h in range(heads):
        dq, dk, dv, dk_far, dv_far = attend_back(
            q_wide, o_wide, g_all, kv_own, kv_far, math.gcd(rows, 1024), h
        )
        dq, q_wide = lax.optimization_barrier((dq, q_wide))
        q_back.append(dq)
        for parts, near, far in ((k_back, dk, dk_far), (v_back, dv, dv_far)):
            total = near.astype(f32)
            for d in range(1, copies):
                total = total + to_copy(far[:, (d - 1) * rows : d * rows], -d).astype(f32)
            parts.append(total.astype(bf16))
    joint_back = jnp.concatenate(
        [value[..., :HD] for value in q_back + k_back + v_back], axis=-1
    ).reshape(seqs * rows, 3 * cols)

    partial = contract_cols(joint_back, w_joint.reshape(width, 3 * cols)).astype(bf16)
    partial = partial.reshape(seqs, groups, span, width)
    input_grad = partial[:, 0].astype(f32) + d_first_sum.reshape(seqs, span, width)
    for d in range(1, groups):
        sent = partial[:, d]
        sent = to_group(sent, -d)
        input_grad = input_grad + sent.astype(f32)

    unscale = jnp.repeat(jnp.array([HD**-0.5, 1.0, 1.0], f32), cols)
    grad_joint = (contract_rows(x_all, joint_back) * unscale).astype(bf16)
    grad_joint = grad_joint.reshape(shards, own_rows, 3 * cols)
    sums = (jnp.sum(joint_back.astype(f32), axis=0) * unscale).reshape(3, cols)
    tail = jnp.zeros((2, width), f32)
    tail = lax.dynamic_update_slice(tail, sums[::2], (0, group * cols))
    tail = tail.reshape(2, shards, own_rows).transpose(1, 0, 2).reshape(shards, 1, -1)
    extra = 32
    tail = jnp.pad(
        tail.astype(bf16), ((0, 0), (0, extra - 1), (0, 3 * cols - tail.shape[-1]))
    )
    grad_joint = jnp.concatenate([grad_joint, tail], axis=1)
    half = reduce_shards(reduce_pair(grad_joint))
    if copies > 2:
        total = half.astype(f32)
        for d in range(2, copies, 2):
            total = total + to_copy(half, d).astype(f32)
        half = total.astype(bf16)
    got = jnp.stack([half] + [to_group(half, d) for d in range(1, groups)])
    got = join_pair(got.transpose(1, 0, 2).reshape(half.shape[0], -1))
    got = got.reshape(own_rows + extra, groups, 3, cols).astype(f32)
    total_joint = jnp.stack(
        [
            lax.dynamic_index_in_dim(got, (group - j) % groups, 1, keepdims=False)
            for j in range(groups)
        ],
        axis=2,
    )[:own_rows].reshape(own_rows, 3 * width)
    biases = jnp.sum(got[own_rows].reshape(groups, -1), axis=0)

    return (
        outputs,
        input_grad,
        total_joint,
        biases[:own_rows],
        biases[own_rows : 2 * own_rows],
        total_output,
        flat[0],
        flat[1],
        flat[2],
        total_hidden,
        flat[6:].reshape(-1),
        total_down,
        flat[3],
        flat[4],
        flat[5],
    )


def solution(mesh):
    placed = (
        P("fsdp", "ctx", None),
        P("fsdp"),
        P("fsdp", "ctx", None),
        P("fsdp", None),
        P("fsdp"),
        P("fsdp"),
        P("fsdp", None),
        P("fsdp"),
        P("fsdp"),
        P("fsdp"),
        P("fsdp", None),
        P("fsdp"),
        P("fsdp", None),
        P("fsdp"),
        P("fsdp"),
        P("fsdp"),
    )

    return jax.shard_map(
        body,
        mesh=mesh,
        in_specs=placed,
        out_specs=(
            P("fsdp", "ctx", None),
            P("fsdp", "ctx", None),
            P("fsdp", None),
            P("fsdp"),
            P("fsdp"),
            P("fsdp", None),
            P("fsdp"),
            P("fsdp"),
            P("fsdp"),
            P("fsdp", None),
            P("fsdp"),
            P("fsdp", None),
            P("fsdp"),
            P("fsdp"),
            P("fsdp"),
        ),
        check_vma=False,
    )
```
